128 devices in a mesh: row: 8 (over y, core), col: 16 (over x, z).
Axes of the slice: x: 4, y: 4, z: 4, core: 2. Of those that a mesh axis runs over, the one named last changes fastest.
Arguments:
- jacobian: bfloat16 [256, 65536], P(('row', 'col')), may hold values from -0.25 to 0.25
- curvature: float32 [256], P(('row', 'col')), may hold values from 0.1 to 10
- sub_index: int32 [65536], P(('row', 'col')), may hold values from 0 to 4194303, as said below
- prior_precision: float32 [32], replicated, may hold values from 0.5 to 4
Outputs:
- factored: float32 [128, 8, 512, 512], P(('row', 'col'))
The draws below stay inside these ranges and needn't reach their ends.
Inputs may be any that keep to these rules, and one draw needn't show every extreme that they name: `sub_index`: strictly increasing along the weights, so each tile holds nearby weights; the first is 0 and the last is 4194303.
All inputs are finite; a program needn't handle non-finite values.
Results may differ from the reference program's by a relative error of at most 0.0025.
Values may be sent and summed in bfloat16 or wider, within the bound.
No kernel may reach another device: no remote copies, remote signals or barrier semaphores. Data moves between devices by JAX's collectives and lax.ppermute only.
A program may use at most 128 MiB of HBM per device.

```python
import math
import jax
import jax.numpy as jnp
from jax import lax

TILE = 512
BAND = 8
PANELS = 1
LAYERS = 32
SPAN = 131072
EXAMPLES = 256
P_SIZE = 65536
NT = 128


def draw_sub_index(key, part):
    count = NT * TILE
    per = count // LAYERS
    spread = max(per // 4, 1)
    jitter = jax.random.randint(jax.random.fold_in(key, 11), (LAYERS - 1,), -spread, spread + 1, dtype=jnp.int32)
    bounds = jnp.arange(1, LAYERS, dtype=jnp.int32) * per + jitter
    weights = jnp.arange(count, dtype=jnp.int32)
    layer = jnp.sum((weights[:, None] >= bounds[None, :]).astype(jnp.int32), axis=1)
    starts = jnp.concatenate([jnp.zeros((1,), jnp.int32), bounds])
    start_of = jnp.sum(jnp.where(layer[:, None] == jnp.arange(LAYERS, dtype=jnp.int32)[None, :], starts[None, :], 0), axis=1)
    parity = jax.random.randint(jax.random.fold_in(key, 23), (count,), 0, 2, dtype=jnp.int32)
    values = layer * SPAN + (weights - start_of) * 2 + parity
    values = values.at[0].set(0)
    values = values.at[count - 1].set(LAYERS * SPAN - 1)
    return values.astype(jnp.int32)


def steps_of(key, dims, pieces, low, largest):
    def one(position, blocks):
        draws = jax.random.uniform(jax.random.fold_in(jax.random.fold_in(key, 6), position), (blocks,), jnp.float32, low / len(pieces), largest / len(pieces))
        return jnp.repeat(jnp.exp(draws), dims[position] // blocks).reshape((-1,) + (1,) * (len(dims) - position - 1))

    level = one(*pieces[0])
    for cut in pieces[1:]:
        level = level * one(*cut)
    return level


def scatter_about(key, extent, width, bound, cuts=(), kind=jnp.bfloat16):
    entries = jax.random.normal(key, extent, jnp.float32) * width
    if len(cuts) > 0:
        entries = steps_of(key, extent, cuts, -0.22, 0.18) * entries
    return jnp.clip(entries, min=-bound, max=bound).astype(kind)


def setup_inputs(seed: int = 0) -> dict:
    key_list = jax.random.split(jax.random.key(seed), 5)
    jacobian = scatter_about(key_list[0], (EXAMPLES, P_SIZE), (2 * EXAMPLES) ** -0.5, 0.25, ((0, 128),))
    curvature = jnp.clip(jnp.exp(math.log(10.0) - 4.6051702 * jax.random.uniform(key_list[1], (EXAMPLES,), jnp.float32) ** steps_of(key_list[1], (EXAMPLES,), ((0, 128),), -0.2, 0.2)), 0.1, 10.0)
    sub_index = draw_sub_index(jax.random.fold_in(key_list[4], 71), 0)
    prior_precision = jnp.clip(jnp.exp(jax.random.uniform(key_list[3], (LAYERS,), jnp.float32, math.log(0.5), math.log(4.0))), 0.5, 4.0)
    return {"jacobian": jacobian, "curvature": curvature, "sub_index": sub_index, "prior_precision": prior_precision}


def reference(jacobian, curvature, sub_index, prior_precision):
    scaled = (jnp.sqrt(curvature)[:, None] * jacobian.astype(jnp.float32)).astype(jnp.bfloat16)
    layer_ids = sub_index // SPAN
    anchor = lax.optimization_barrier(jnp.sum(jnp.where(layer_ids[:, None] == jnp.arange(LAYERS, dtype=jnp.int32)[None, :], prior_precision[None, :], jnp.float32(0.0)), axis=1))
    padded = jnp.concatenate([jnp.zeros((EXAMPLES, (BAND - 1) * TILE), jnp.bfloat16), scaled], axis=1)
    identity = jnp.eye(TILE, dtype=jnp.float32)
    band_index = jnp.arange(BAND, dtype=jnp.int32)

    def one_row(tile_id):
        start = tile_id * TILE
        own_tiles = lax.dynamic_slice_in_dim(scaled, start, TILE, 1)
        window_tiles = lax.dynamic_slice_in_dim(padded, start, BAND * TILE, 1)
        product = lax.dot_general(own_tiles.astype(jnp.float32), window_tiles.astype(jnp.float32), (((0,), (0,)), ((), ())), preferred_element_type=jnp.float32)
        blocks = product.reshape(TILE, BAND, TILE)[:, ::-1, :].transpose(1, 0, 2)
        in_group = band_index <= tile_id % BAND
        blocks = jnp.where(in_group[:, None, None], blocks, jnp.float32(0.0))
        diagonal = lax.dynamic_slice_in_dim(anchor, start, TILE, 0)
        return blocks.at[0].add(identity * diagonal[:, None])
    band_tiles = lax.map(one_row, jnp.arange(NT, dtype=jnp.int32))
    groups = band_tiles.reshape(NT // BAND, BAND, BAND, TILE, TILE)
    for panel in range(PANELS):
        factor_tile = jnp.linalg.cholesky(groups[:, panel, 0])
        solved = [factor_tile]
        for offset in range(1, BAND - panel):
            solved.append(lax.linalg.triangular_solve(factor_tile, groups[:, panel + offset, offset], left_side=False, lower=True, transpose_a=True))
        for offset in range(1, BAND - panel):
            for other in range(1, offset + 1):
                term = jnp.matmul(solved[offset], jnp.swapaxes(solved[other], 1, 2), precision=lax.Precision.HIGHEST)
                groups = groups.at[:, panel + offset, offset - other].add(-term)
        groups = groups.at[:, panel, 0].set(factor_tile)
        for offset in range(1, BAND - panel):
            groups = groups.at[:, panel + offset, offset].set(solved[offset])
    return groups.reshape(NT, BAND, TILE, TILE)
```

```python
import jax
import jax.numpy as jnp
from jax import lax
from jax.experimental import pallas as pl
from jax.experimental.pallas import tpu as pltpu
from jax.sharding import PartitionSpec as P

TILE = 512
BAND = 8
LAYERS = 32
SPAN = 131072
GROUPS = 16
DEVICES = 128
EXAMPLES = 256
WIDE = TILE + 128
REST = (BAND - 1) * TILE
PART = 128
F32 = jnp.float32
BF16 = jnp.bfloat16
AXES = ("row", "col")
VMEM_LIMIT = 56 * 1024 * 1024


def params():
    return pltpu.CompilerParams(vmem_limit_bytes=VMEM_LIMIT)


def halves(x):
    high = x.astype(BF16)
    return high, (x - high.astype(F32)).astype(BF16)


def thirds(x):
    high = x.astype(BF16)
    rest = x - high.astype(F32)
    mid = rest.astype(BF16)
    return high, mid, (rest - mid.astype(F32)).astype(BF16)


def dot(a, b, contract):
    return lax.dot_general(a, b, ((contract[0], contract[1]), ((), ())), preferred_element_type=F32)


def dot_full(a, b, contract):
    return lax.dot_general(
        a, b, ((contract[0], contract[1]), ((), ())),
        precision=lax.Precision.HIGHEST, preferred_element_type=F32,
    )


def root_curvature(curvature_ref, width):
    rows = lax.broadcasted_iota(jnp.int32, (2, width), 0)
    return jnp.sqrt(jnp.where(rows == 0, curvature_ref[0], curvature_ref[1]))


def first_kernel(curvature_ref, jacobian_ref, index_ref, out_ref, held, sems):
    root = root_curvature(curvature_ref, TILE)
    slot = lax.broadcasted_iota(jnp.int32, (PART, TILE), 0)
    layer = jnp.where(slot < LAYERS, slot, slot - (LAYERS - 1))
    below = (index_ref[...] < layer * SPAN).astype(F32)
    counts = jnp.sum(below, axis=1, keepdims=True)
    eye = lax.broadcasted_iota(jnp.int32, (PART, PART), 0) == lax.broadcasted_iota(jnp.int32, (PART, PART), 1)
    counts = jnp.sum(jnp.where(eye, counts, 0.0), axis=0, keepdims=True)
    high = jnp.floor(counts * (1.0 / 32.0))
    low = counts - 32.0 * high
    rows = lax.broadcasted_iota(jnp.int32, (2, PART), 0)
    tail = jnp.where(rows == 0, high, low).astype(BF16)
    for g in range(GROUPS):
        block = jacobian_ref[:, g * BAND * TILE : g * BAND * TILE + TILE].astype(F32)
        held[g, :, :TILE] = (root * block).astype(BF16)
        held[g, :, TILE:] = tail
    copies = [pltpu.make_async_copy(held, out_ref.at[:, i], sems.at[i]) for i in range(BAND)]
    for copy in copies:
        copy.start()
    for copy in copies:
        copy.wait()


def rest_kernel(curvature_ref, jacobian_ref, out_ref, held, sems):
    root = root_curvature(curvature_ref, REST)
    for g in range(GROUPS):
        block = jacobian_ref[:, g * BAND * TILE + TILE : (g + 1) * BAND * TILE].astype(F32)
        held[g] = (root * block).astype(BF16)
    copies = [pltpu.make_async_copy(held, out_ref.at[:, i], sems.at[i]) for i in range(BAND)]
    for copy in copies:
        copy.start()
    for copy in copies:
        copy.wait()


def factor_part(v_ref):
    sub = lax.broadcasted_iota(jnp.int32, (8, PART), 0)
    steps = PART // 8

    def rows_at(k):
        x = v_ref[8 * k : 8 * k + 8, :]
        return [x[:, :PART], x[:, PART:]]

    def columns(x, k):
        return [jnp.broadcast_to(x[0][:, 8 * k + c : 8 * k + c + 1], (8, PART)) for c in range(8)]

    ahead = {}
    for k in range(steps):
        now = ahead.pop(k) if k in ahead else rows_at(k)
        look = [n for n in (k + 1, k + 2) if n < steps]
        later = {n: (ahead[n] if n in ahead else rows_at(n)) for n in look}
        pivot = columns(now, k)
        below = {n: columns(later[n], k) for n in look}
        scale = jnp.zeros((8, PART), F32)
        for i in range(8):
            value = jnp.broadcast_to(pivot[i][i : i + 1, :], (8, PART))
            inverse = 1.0 / value
            scale = jnp.where(sub == i, value, scale)
            factor = jnp.where(sub > i, pivot[i] * inverse, 0.0)
            factors = {n: below[n][i] * inverse for n in look}
            for c in range(i + 1, 8):
                row = jnp.broadcast_to(pivot[c][i : i + 1, :], (8, PART))
                pivot[c] = pivot[c] - factor * row
                for n in look:
                    below[n][c] = below[n][c] - factors[n] * row
            for h in range(2):
                row = jnp.broadcast_to(now[h][i : i + 1, :], (8, PART))
                now[h] = now[h] - factor * row
                for n in look:
                    later[n][h] = later[n][h] - factors[n] * row
        root = lax.rsqrt(scale)
        done = jnp.concatenate([now[0] * root, now[1] * root], axis=1)
        v_ref[8 * k : 8 * k + 8, :] = done
        ahead.update(later)
        start = 8 * (k + 3)
        if start < PART:
            high, mid, low = thirds(done)
            left = jnp.concatenate([high, high, mid, high, low, mid], axis=0)[:, :PART]
            right = jnp.concatenate([high, mid, high, low, high, mid], axis=0)
            change = dot(left, right, ((0,), (0,)))
            v_ref[start:, :] = v_ref[start:, :] - change[start:, :]


def tile_of(block):
    return block.reshape(EXAMPLES, TILE)


def panel_kernel(lead_ref, first_ref, prior_ref, zt_ref, w_ref, diag_ref, g_ref, v_ref):
    tile = tile_of(first_ref[:, :, :TILE])
    note = first_ref[pl.ds(lead_ref[0], 1), :, TILE:].reshape(2, PART).astype(F32)
    note = 32.0 * note[0:1, :] + note[1:2, :]
    r32 = lax.broadcasted_iota(jnp.int32, (LAYERS, PART), 0)
    c32 = lax.broadcasted_iota(jnp.int32, (LAYERS, PART), 1)
    low = jnp.sum(jnp.where(c32 == r32, note, 0.0), axis=1, keepdims=True)
    high = jnp.sum(jnp.where(c32 == r32 + LAYERS, note, 0.0), axis=1, keepdims=True)
    at = lax.broadcasted_iota(jnp.int32, (LAYERS, TILE), 1).astype(F32)
    inside = (at >= low) & (at < high)
    anchor = jnp.sum(jnp.where(inside, prior_ref[...], 0.0), axis=0, keepdims=True)

    row = lax.broadcasted_iota(jnp.int32, (TILE, TILE), 0)
    column = lax.broadcasted_iota(jnp.int32, (TILE, TILE), 1)
    gram = dot(tile, tile, ((0,), (0,)))
    g_ref[:, :TILE] = jnp.where(row == column, gram + anchor, gram)
    g_ref[:, TILE:] = tile.astype(F32).T
    r128 = lax.broadcasted_iota(jnp.int32, (PART, PART), 0)
    c128 = lax.broadcasted_iota(jnp.int32, (PART, PART), 1)
    eye = (r128 == c128).astype(F32)
    parts = TILE // PART
    for b in range(parts):
        at_rows = slice(b * PART, (b + 1) * PART)
        after = (b + 1) * PART
        v_ref[:, :PART] = g_ref[at_rows, at_rows]
        v_ref[:, PART:] = eye
        factor_part(v_ref)
        diag_ref[at_rows, :] = jnp.where(r128 <= c128, v_ref[:, :PART], 0.0).T
        solved = dot_full(v_ref[:, PART:], g_ref[at_rows, after:], ((1,), (0,)))
        zt_ref[at_rows, :] = solved[:, TILE - after :]
        if b < parts - 1:
            change = dot_full(solved[:, : TILE - after], solved, ((0,), (0,)))
            g_ref[after:, after:] = g_ref[after:, after:] - change
    zt = zt_ref[...]
    r256 = lax.broadcasted_iota(jnp.int32, (EXAMPLES, EXAMPLES), 0)
    c256 = lax.broadcasted_iota(jnp.int32, (EXAMPLES, EXAMPLES), 1)
    w_ref[...] = (r256 == c256).astype(F32) - dot_full(zt, zt, ((0,), (0,)))


def band_kernel(place_ref, first_ref, rest_ref, zt_ref, w_ref, diag_ref, index_ref, prior_ref, out_ref, vh, vl, q_ref):
    place = place_ref[0]
    k = pl.program_id(0)

    @pl.when(k == 0)
    def _():
        def fill(own):
            zh, zl = halves(zt_ref[...])
            q_ref[...] = dot(own, zh, ((0,), (1,))) + dot(own, zl, ((0,), (1,)))

        @pl.when(place == 0)
        def _():
            fill(tile_of(first_ref[:, :, :TILE]))
            q = q_ref[...]
            row = lax.broadcasted_iota(jnp.int32, (TILE, TILE), 0) // PART
            column = lax.broadcasted_iota(jnp.int32, (TILE, TILE), 1) // PART
            diag = jnp.concatenate([diag_ref[...]] * (TILE // PART), axis=1)
            q_ref[...] = jnp.where(row == column, diag, jnp.where(row > column, q, 0.0))

        @pl.when(place > 0)
        def _():
            start = pl.multiple_of((place - 1) * TILE, TILE)
            own = tile_of(rest_ref[:, :, pl.ds(start, TILE)])
            fill(own)
            wh, wl = halves(w_ref[...])
            v = dot(own, wh, ((0,), (0,))) + dot(own, wl, ((0,), (0,)))
            vh[...], vl[...] = halves(v)

    @pl.when(k < place)
    def _():
        start = pl.multiple_of((place - k - 1) * TILE, TILE)
        other = tile_of(rest_ref[:, :, pl.ds(start, TILE)])
        out_ref[0, 0] = dot(vh[...], other, ((1,), (0,))) + dot(vl[...], other, ((1,), (0,)))

    @pl.when((k == 0) & (place > 0))
    def _():
        layer = lax.broadcasted_iota(jnp.int32, (LAYERS, TILE), 0) * SPAN
        index = index_ref[...]
        inside = (index >= layer) & (index < layer + SPAN)
        anchor = jnp.sum(jnp.where(inside, prior_ref[...], 0.0), axis=0, keepdims=True)
        row = lax.broadcasted_iota(jnp.int32, (TILE, TILE), 0)
        column = lax.broadcasted_iota(jnp.int32, (TILE, TILE), 1)
        out_ref[0, 0] = out_ref[0, 0] + jnp.where(row == column, anchor, 0.0)

    @pl.when(k == place)
    def _():
        out_ref[0, 0] = q_ref[...]

    @pl.when(k > place)
    def _():
        out_ref[0, 0] = jnp.zeros((TILE, TILE), F32)


SMEM = pl.BlockSpec(memory_space=pltpu.SMEM)
VMEM = pl.BlockSpec(memory_space=pltpu.VMEM)
HBM = pl.BlockSpec(memory_space=pl.ANY)


def body(jacobian, curvature, sub_index, prior_precision):
    position = lax.axis_index(AXES).astype(jnp.int32)
    index = sub_index.reshape(1, TILE)
    prior = prior_precision.reshape(LAYERS, 1)
    send_first = pl.pallas_call(
        first_kernel,
        out_shape=jax.ShapeDtypeStruct((GROUPS, BAND, 2, WIDE), BF16),
        in_specs=[SMEM, VMEM, VMEM],
        out_specs=HBM,
        scratch_shapes=[pltpu.VMEM((GROUPS, 2, WIDE), BF16), pltpu.SemaphoreType.DMA((BAND,))],
        compiler_params=params(),
        name="first_send",
    )(curvature, jacobian, index)
    first = lax.all_to_all(
        send_first.reshape(DEVICES, 2, WIDE), AXES, split_axis=0, concat_axis=0, tiled=True
    )
    send_rest = pl.pallas_call(
        rest_kernel,
        out_shape=jax.ShapeDtypeStruct((GROUPS, BAND, 2, REST), BF16),
        in_specs=[SMEM, VMEM],
        out_specs=HBM,
        scratch_shapes=[pltpu.VMEM((GROUPS, 2, REST), BF16), pltpu.SemaphoreType.DMA((BAND,))],
        compiler_params=params(),
        name="rest_send",
    )(curvature, jacobian)
    send_rest, first = lax.optimization_barrier((send_rest, first))
    rest = lax.all_to_all(
        send_rest.reshape(DEVICES, 2, REST), AXES, split_axis=0, concat_axis=0, tiled=True
    )
    zt, w, diag = pl.pallas_call(
        panel_kernel,
        out_shape=[
            jax.ShapeDtypeStruct((TILE, EXAMPLES), F32),
            jax.ShapeDtypeStruct((EXAMPLES, EXAMPLES), F32),
            jax.ShapeDtypeStruct((TILE, PART), F32),
        ],
        in_specs=[SMEM, VMEM, VMEM],
        out_specs=[VMEM, VMEM, VMEM],
        scratch_shapes=[pltpu.VMEM((TILE, TILE + EXAMPLES), F32), pltpu.VMEM((PART, 2 * PART), F32)],
        compiler_params=params(),
        cost_estimate=pl.CostEstimate(flops=2 * 10**10, bytes_accessed=2 * 10**6, transcendentals=10**6),
        name="panel",
    )((position // BAND * BAND).reshape(1), first, prior)
    whole = lambda *shape: pl.BlockSpec(shape, lambda k: (0,) * len(shape))
    return pl.pallas_call(
        band_kernel,
        grid=(BAND,),
        out_shape=jax.ShapeDtypeStruct((1, BAND, TILE, TILE), F32),
        in_specs=[
            SMEM,
            whole(DEVICES, 2, WIDE),
            whole(DEVICES, 2, REST),
            whole(TILE, EXAMPLES),
            whole(EXAMPLES, EXAMPLES),
            whole(TILE, PART),
            whole(1, TILE),
            whole(LAYERS, 1),
        ],
        out_specs=pl.BlockSpec((1, 1, TILE, TILE), lambda k: (0, k, 0, 0)),
        scratch_shapes=[
            pltpu.VMEM((TILE, EXAMPLES), BF16),
            pltpu.VMEM((TILE, EXAMPLES), BF16),
            pltpu.VMEM((TILE, TILE), F32),
        ],
        compiler_params=params(),
        name="band",
    )((position % BAND).reshape(1), first, rest, zt, w, diag, index, prior)


def solution(mesh):
    placed = (P(AXES, None), P(AXES), P(AXES), P())
    return jax.shard_map(
        body,
        mesh=mesh,
        in_specs=placed,
        out_specs=P(AXES, None, None, None),
        check_vma=False,
    )
```

```python
import jax
import jax.numpy as jnp
from jax import lax
from jax.experimental import pallas as pl
from jax.experimental.pallas import tpu as pltpu
from jax.sharding import PartitionSpec as P

TILE = 512
BAND = 8
LAYERS = 32
SPAN = 131072
GROUPS = 16
DEVICES = 128
EXAMPLES = 256
WIDE = TILE + 128
REST = (BAND - 2) * TILE
PART = 128
F32 = jnp.float32
BF16 = jnp.bfloat16
AXES = ("row", "col")
VMEM_LIMIT = 56 * 1024 * 1024


def params():
    return pltpu.CompilerParams(vmem_limit_bytes=VMEM_LIMIT)


def halves(x):
    high = x.astype(BF16)
    return high, (x - high.astype(F32)).astype(BF16)


def thirds(x):
    high = x.astype(BF16)
    rest = x - high.astype(F32)
    mid = rest.astype(BF16)
    return high, mid, (rest - mid.astype(F32)).astype(BF16)


def dot(a, b, contract):
    return lax.dot_general(a, b, ((contract[0], contract[1]), ((), ())), preferred_element_type=F32)


def dot_wide(a, b, axis):
    ah, al = halves(a)
    bh, bl = halves(b)
    left = jnp.concatenate([ah, ah, al], axis=axis)
    right = jnp.concatenate([bh, bl, bh], axis=0)
    return dot(left, right, ((axis,), (0,)))


def root_curvature(curvature_ref, width):
    rows = lax.broadcasted_iota(jnp.int32, (2, width), 0)
    return jnp.sqrt(jnp.where(rows == 0, curvature_ref[0], curvature_ref[1]))


def first_kernel(curvature_ref, jacobian_ref, index_ref, out_ref, shared, own, sems):
    root = root_curvature(curvature_ref, BAND * TILE)
    slot = lax.broadcasted_iota(jnp.int32, (PART, TILE), 0)
    layer = jnp.where(slot < LAYERS, slot, slot - (LAYERS - 1))
    below = (index_ref[...] < layer * SPAN).astype(F32)
    counts = jnp.sum(below, axis=1, keepdims=True)
    eye = lax.broadcasted_iota(jnp.int32, (PART, PART), 0) == lax.broadcasted_iota(jnp.int32, (PART, PART), 1)
    counts = jnp.sum(jnp.where(eye, counts, 0.0), axis=0, keepdims=True)
    high = jnp.floor(counts * (1.0 / 32.0))
    low = counts - 32.0 * high
    rows = lax.broadcasted_iota(jnp.int32, (2, PART), 0)
    tail = jnp.where(rows == 0, high, low).astype(BF16)
    for g in range(GROUPS):
        block = jacobian_ref[:, g * BAND * TILE : (g + 1) * BAND * TILE].astype(F32)
        block = (root * block).astype(BF16)
        shared[g, :, :TILE] = block[:, :TILE]
        shared[g, :, TILE:] = tail
        for i in range(BAND):
            own[g, i] = block[:, i * TILE : (i + 1) * TILE]
    copies = [
        pltpu.make_async_copy(shared, out_ref.at[:, i, :, pl.ds(0, WIDE)], sems.at[i])
        for i in range(BAND)
    ]
    copies.append(pltpu.make_async_copy(own, out_ref.at[:, :, :, pl.ds(WIDE, TILE)], sems.at[BAND]))
    for copy in copies:
        copy.start()
    for copy in copies:
        copy.wait()


def rest_kernel(curvature_ref, jacobian_ref, out_ref, held, sems):
    root = root_curvature(curvature_ref, REST)
    for g in range(GROUPS):
        start = g * BAND * TILE + TILE
        block = jacobian_ref[:, start : start + REST].astype(F32)
        held[g] = (root * block).astype(BF16)
    copies = [pltpu.make_async_copy(held, out_ref.at[:, i], sems.at[i]) for i in range(BAND)]
    for copy in copies:
        copy.start()
    for copy in copies:
        copy.wait()


def factor_part(v_ref, d_ref):
    sub = lax.broadcasted_iota(jnp.int32, (8, PART), 0)
    lane = lax.broadcasted_iota(jnp.int32, (8, PART), 1)
    steps = PART // 8

    def spread(x):
        return jnp.broadcast_to(x, (8, PART))

    def rows_at(k):
        return v_ref[8 * k : 8 * k + 8, :]

    def columns(x, k):
        return [spread(x[:, 8 * k + c : 8 * k + c + 1]) for c in range(8)]

    held = {k: rows_at(k) for k in range(3)}
    pivot = columns(held[0], 0)
    near = columns(held[1], 0)
    for k in range(steps):
        now, one, two = held.pop(k), held.get(k + 1), held.get(k + 2)
        far = columns(two, k) if two is not None else None
        next_pivot = columns(one, k + 1) if one is not None else None
        next_near = columns(two, k + 1) if two is not None else None
        here = (lane >= 8 * k) & (lane < 8 * k + 8)
        now = jnp.where(here, (lane - 8 * k == sub).astype(F32), now)
        if one is not None:
            one = jnp.where(here, 0.0, one)
        if two is not None:
            two = jnp.where(here, 0.0, two)
        scale = jnp.zeros((8, PART), F32)
        for i in range(8):
            value = spread(pivot[i][i : i + 1])
            inverse = 1.0 / value
            scale = jnp.where(sub == i, value, scale)
            f0 = jnp.where(sub > i, pivot[i] * inverse, 0.0)
            f1 = near[i] * inverse if one is not None else None
            f2 = far[i] * inverse if two is not None else None
            for c in range(i + 1, 8):
                row = spread(pivot[c][i : i + 1])
                pivot[c] = pivot[c] - f0 * row
                if one is not None:
                    near[c] = near[c] - f1 * row
                if two is not None:
                    far[c] = far[c] - f2 * row
            if one is not None:
                for c in range(8):
                    row = spread(near[i][c : c + 1])
                    next_pivot[c] = next_pivot[c] - f1 * row
                    if two is not None:
                        next_near[c] = next_near[c] - f2 * row
            row = spread(now[i : i + 1])
            now = now - f0 * row
            if one is not None:
                one = one - f1 * row
            if two is not None:
                two = two - f2 * row
        root = lax.rsqrt(scale)
        done = now * root
        v_ref[8 * k : 8 * k + 8, :] = done
        block = jnp.zeros((8, PART), F32)
        for c in range(8):
            block = jnp.where((lane == 8 * k + c) & (sub <= c), pivot[c], block)
        d_ref[8 * k : 8 * k + 8, :] = block * root
        if one is not None:
            held[k + 1] = one
        if two is not None:
            held[k + 2] = two
        pivot, near = next_pivot, next_near
        start = 8 * (k + 3)
        if start < PART:
            high, mid, low = thirds(done)
            left = jnp.concatenate([high, high, mid, high, low, mid], axis=0)
            right = jnp.concatenate([high, mid, high, low, high, mid], axis=0)
            change = dot(left, right, ((0,), (0,)))
            at = lax.broadcasted_iota(jnp.int32, (PART - start, PART), 1)
            keep = jnp.where((at >= 8 * k) & (at < 8 * k + 8), 0.0, v_ref[start:, :])
            v_ref[start:, :] = keep - change[start:, :]
            held[k + 3] = rows_at(k + 3)


def tile_of(block):
    return block.reshape(EXAMPLES, TILE)


def layer_anchor(low, high, at, prior_ref):
    inside = (at >= low) & (at < high)
    return jnp.sum(jnp.where(inside, prior_ref[...], 0.0), axis=0, keepdims=True)


def panel_kernel(info_ref, first_ref, index_ref, prior_ref, out_ref, v_ref, *scratch):
    parts = TILE // PART
    r_refs, (t_ref, f_ref, d_ref, made, zero, sems) = scratch[:parts], scratch[parts:]
    lead, place = info_ref[0], info_ref[1]

    def store(source, k):
        return pltpu.make_async_copy(source, out_ref.at[0, k], sems.at[k])

    zero[...] = jnp.zeros((TILE, TILE), F32)
    for k in range(1, BAND):
        @pl.when(k > place)
        def _():
            store(zero, k).start()

    tile = tile_of(first_ref[:, :, :TILE])
    own = tile_of(first_ref[:, :, WIDE:])
    own2 = jnp.concatenate([own, own], axis=0)
    note = first_ref[pl.ds(lead, 1), :, TILE:WIDE].reshape(2, PART).astype(F32)
    note = 32.0 * note[0:1, :] + note[1:2, :]
    r32 = lax.broadcasted_iota(jnp.int32, (LAYERS, PART), 0)
    c32 = lax.broadcasted_iota(jnp.int32, (LAYERS, PART), 1)
    low = jnp.sum(jnp.where(c32 == r32, note, 0.0), axis=1, keepdims=True)
    high = jnp.sum(jnp.where(c32 == r32 + LAYERS, note, 0.0), axis=1, keepdims=True)
    at = lax.broadcasted_iota(jnp.int32, (LAYERS, TILE), 1).astype(F32)
    anchor = layer_anchor(low, high, at, prior_ref)

    r128 = lax.broadcasted_iota(jnp.int32, (PART, PART), 0)
    c128 = lax.broadcasted_iota(jnp.int32, (PART, PART), 1)
    turned = tile.astype(F32).T
    for b in range(parts):
        block = slice(b * PART, (b + 1) * PART)
        gram = dot(tile[:, block], tile[:, b * PART :], ((0,), (0,)))
        t_ref[b] = gram[:, :PART] + jnp.where(r128 == c128, anchor[:, block], 0.0)
        if b < parts - 1:
            r_refs[b][:, : TILE - (b + 1) * PART] = gram[:, PART:]
        r_refs[b][:, TILE - (b + 1) * PART :] = turned[block, :]

    r256 = lax.broadcasted_iota(jnp.int32, (EXAMPLES, EXAMPLES), 0)
    c256 = lax.broadcasted_iota(jnp.int32, (EXAMPLES, EXAMPLES), 1)
    w = (r256 == c256).astype(F32)
    for b in range(parts):
        block = slice(b * PART, (b + 1) * PART)
        after = (b + 1) * PART
        f_ref[b] = t_ref[b]
        factor_part(f_ref.at[b], d_ref.at[b])
        f = f_ref[b]
        inverse = jnp.where(c128 // 8 <= r128 // 8, f, 0.0)
        d_ref[b] = jnp.where(c128 // 8 > r128 // 8, f, d_ref[b])
        if b < parts - 1:
            first = dot_wide(inverse, r_refs[b][:, :PART], 1)
            t_ref[b + 1] = t_ref[b + 1] - dot_wide(first, first, 0)
            others = dot_wide(inverse, r_refs[b][:, PART:], 1)
            solved = jnp.concatenate([first, others], axis=1)
            for c in range(b + 1, parts):
                skip = (c - b - 1) * PART
                change = dot_wide(solved[:, skip : skip + PART], solved[:, skip:], 0)
                if c > b + 1:
                    t_ref[c] = t_ref[c] - change[:, :PART]
                r_refs[c][...] = r_refs[c][...] - change[:, PART:]
        else:
            solved = dot_wide(inverse, r_refs[b][...], 1)
        zt = solved[:, TILE - after :]
        z2 = jnp.concatenate(halves(zt), axis=1)
        made[1, :, block] = dot(own2, z2, ((0,), (1,)))
        w = w - dot_wide(zt, zt, 0)

    @pl.when(place == 0)
    def _():
        for b in range(parts):
            block = slice(b * PART, (b + 1) * PART)
            if b > 0:
                made[1, : b * PART, block] = jnp.zeros((b * PART, PART), F32)
            made[1, block, block] = d_ref[b].T

    store(made.at[1], place).start()
    w2 = jnp.concatenate(halves(w), axis=0)
    v = jnp.concatenate(halves(dot(own2, w2, ((0,), (0,)))), axis=1)
    v_ref[...] = v

    @pl.when(place > 0)
    def _():
        layer = lax.broadcasted_iota(jnp.int32, (LAYERS, TILE), 0) * SPAN
        own_anchor = layer_anchor(layer, layer + SPAN, index_ref[...], prior_ref)
        row = lax.broadcasted_iota(jnp.int32, (TILE, TILE), 0)
        column = lax.broadcasted_iota(jnp.int32, (TILE, TILE), 1)
        made[0] = dot(v_ref[...], own2, ((1,), (0,))) + jnp.where(row == column, own_anchor, 0.0)
        store(made.at[0], 0).start()
        store(made.at[0], 0).wait()

    store(made.at[1], place).wait()
    for k in range(1, BAND):
        @pl.when(k > place)
        def _():
            store(zero, k).wait()


def band_kernel(place_ref, v_ref, rest_ref, before_ref, out_ref, made, sems):
    place = place_ref[0]

    def store(k):
        return pltpu.make_async_copy(made.at[k - 1], out_ref.at[0, k], sems.at[k - 1])

    for k in range(1, BAND - 1):
        @pl.when(k < place)
        def _():
            start = pl.multiple_of((place - k - 1) * TILE, TILE)
            other = tile_of(rest_ref[:, :, pl.ds(start, TILE)])
            made[k - 1] = dot(v_ref[...], jnp.concatenate([other, other], axis=0), ((1,), (0,)))
            store(k).start()

    for k in range(1, BAND - 1):
        @pl.when(k < place)
        def _():
            store(k).wait()


SMEM = pl.BlockSpec(memory_space=pltpu.SMEM)
VMEM = pl.BlockSpec(memory_space=pltpu.VMEM)
HBM = pl.BlockSpec(memory_space=pl.ANY)


def body(jacobian, curvature, sub_index, prior_precision):
    position = lax.axis_index(AXES).astype(jnp.int32)
    place = lax.rem(position, BAND)
    index = sub_index.reshape(1, TILE)
    prior = prior_precision.reshape(LAYERS, 1)
    send_first = pl.pallas_call(
        first_kernel,
        out_shape=jax.ShapeDtypeStruct((GROUPS, BAND, 2, WIDE + TILE), BF16),
        in_specs=[SMEM, VMEM, VMEM],
        out_specs=HBM,
        scratch_shapes=[
            pltpu.VMEM((GROUPS, 2, WIDE), BF16),
            pltpu.VMEM((GROUPS, BAND, 2, TILE), BF16),
            pltpu.SemaphoreType.DMA((BAND + 1,)),
        ],
        compiler_params=params(),
        name="first_send",
    )(curvature, jacobian, index)
    first = lax.all_to_all(
        send_first.reshape(DEVICES, 2, WIDE + TILE), AXES, split_axis=0, concat_axis=0, tiled=True
    )
    send_rest = pl.pallas_call(
        rest_kernel,
        out_shape=jax.ShapeDtypeStruct((GROUPS, BAND, 2, REST), BF16),
        in_specs=[SMEM, VMEM],
        out_specs=HBM,
        scratch_shapes=[pltpu.VMEM((GROUPS, 2, REST), BF16), pltpu.SemaphoreType.DMA((BAND,))],
        compiler_params=params(),
        name="rest_send",
    )(curvature, jacobian)
    send_rest, first = lax.optimization_barrier((send_rest, first))
    rest = lax.all_to_all(
        send_rest.reshape(DEVICES, 2, REST), AXES, split_axis=0, concat_axis=0, tiled=True
    )
    parts = TILE // PART
    before, v = pl.pallas_call(
        panel_kernel,
        out_shape=[
            jax.ShapeDtypeStruct((1, BAND, TILE, TILE), F32),
            jax.ShapeDtypeStruct((TILE, 2 * EXAMPLES), BF16),
        ],
        in_specs=[SMEM, VMEM, VMEM, VMEM],
        out_specs=[HBM, VMEM],
        scratch_shapes=[pltpu.VMEM((PART, TILE - (b + 1) * PART + EXAMPLES), F32) for b in range(parts)]
        + [
            pltpu.VMEM((parts, PART, PART), F32),
            pltpu.VMEM((parts, PART, PART), F32),
            pltpu.VMEM((parts, PART, PART), F32),
            pltpu.VMEM((2, TILE, TILE), F32),
            pltpu.VMEM((TILE, TILE), F32),
            pltpu.SemaphoreType.DMA((BAND,)),
        ],
        compiler_params=params(),
        cost_estimate=pl.CostEstimate(flops=2 * 10**10, bytes_accessed=2 * 10**6, transcendentals=10**6),
        name="panel",
    )(jnp.stack([position - place, place]), pltpu.with_memory_space_constraint(first, pltpu.VMEM), index, prior)
    return pl.pallas_call(
        band_kernel,
        out_shape=jax.ShapeDtypeStruct((1, BAND, TILE, TILE), F32),
        in_specs=[SMEM, VMEM, VMEM, HBM],
        out_specs=HBM,
        scratch_shapes=[
            pltpu.VMEM((BAND - 2, TILE, TILE), F32),
            pltpu.SemaphoreType.DMA((BAND - 2,)),
        ],
        input_output_aliases={3: 0},
        compiler_params=params(),
        name="band",
    )(place.reshape(1), v, pltpu.with_memory_space_constraint(rest, pltpu.VMEM), before)


def solution(mesh):
    placed = (P(AXES, None), P(AXES), P(AXES), P())
    return jax.shard_map(
        body,
        mesh=mesh,
        in_specs=placed,
        out_specs=P(AXES, None, None, None),
        check_vma=False,
    )
```

```python
import jax
import jax.numpy as jnp
from jax import lax
from jax.experimental import pallas as pl
from jax.experimental.pallas import tpu as pltpu
from jax.sharding import PartitionSpec as P

TILE = 512
BAND = 8
LAYERS = 32
SPAN = 131072
GROUPS = 16
DEVICES = 128
EXAMPLES = 256
WIDE = TILE + 128
REST = (BAND - 3) * TILE
PART = 128
F32 = jnp.float32
BF16 = jnp.bfloat16
AXES = ("row", "col")
VMEM_LIMIT = 56 * 1024 * 1024


def params():
    return pltpu.CompilerParams(vmem_limit_bytes=VMEM_LIMIT)


def halves(x):
    high = x.astype(BF16)
    return high, (x - high.astype(F32)).astype(BF16)


def dot(a, b, contract):
    return lax.dot_general(a, b, ((contract[0], contract[1]), ((), ())), preferred_element_type=F32)


def dot_wide(a, b, axis):
    ah, al = halves(a)
    bh, bl = halves(b)
    left = jnp.concatenate([ah, ah, al], axis=axis)
    right = jnp.concatenate([bh, bl, bh], axis=0)
    return dot(left, right, ((axis,), (0,)))


def root_curvature(curvature_ref, width):
    rows = lax.broadcasted_iota(jnp.int32, (2, width), 0)
    return jnp.sqrt(jnp.where(rows == 0, curvature_ref[0], curvature_ref[1]))


def first_kernel(curvature_ref, jacobian_ref, index_ref, out_ref):
    root = root_curvature(curvature_ref, BAND * TILE)
    slot = lax.broadcasted_iota(jnp.int32, (PART, TILE), 0)
    layer = jnp.where(slot < LAYERS, slot, slot - (LAYERS - 1))
    below = (index_ref[...] < layer * SPAN).astype(F32)
    counts = jnp.sum(below, axis=1, keepdims=True)
    eye = lax.broadcasted_iota(jnp.int32, (PART, PART), 0) == lax.broadcasted_iota(jnp.int32, (PART, PART), 1)
    counts = jnp.sum(jnp.where(eye, counts, 0.0), axis=0, keepdims=True)
    high = jnp.floor(counts * (1.0 / 32.0))
    low = counts - 32.0 * high
    rows = lax.broadcasted_iota(jnp.int32, (2, PART), 0)
    tail = jnp.where(rows == 0, high, low).astype(BF16)
    for g in range(GROUPS):
        block = jacobian_ref[:, g * BAND * TILE : (g + 1) * BAND * TILE].astype(F32)
        block = (root * block).astype(BF16)
        for i in range(BAND):
            out_ref[g, i, :, :TILE] = block[:, :TILE]
            out_ref[g, i, :, TILE:WIDE] = tail
            out_ref[g, i, :, WIDE:] = block[:, i * TILE : (i + 1) * TILE]


def rest_kernel(curvature_ref, jacobian_ref, out_ref, held, sems):
    root = root_curvature(curvature_ref, REST)
    for g in range(GROUPS):
        start = g * BAND * TILE + TILE
        block = jacobian_ref[:, start : start + REST].astype(F32)
        held[g] = (root * block).astype(BF16)
    copies = [pltpu.make_async_copy(held, out_ref.at[:, i], sems.at[i]) for i in range(BAND)]
    for copy in copies:
        copy.start()
    for copy in copies:
        copy.wait()


def factor_part(v_ref):
    sub = lax.broadcasted_iota(jnp.int32, (8, PART), 0)
    lane = lax.broadcasted_iota(jnp.int32, (8, PART), 1)
    steps = PART // 8

    def spread(x):
        return jnp.broadcast_to(x, (8, PART))

    def rows_at(k):
        return v_ref[8 * k : 8 * k + 8, :]

    def columns(x, k):
        return [spread(x[:, 8 * k + c : 8 * k + c + 1]) for c in range(8)]

    held = {k: rows_at(k) for k in range(3)}
    pivot = columns(held[0], 0)
    near = columns(held[1], 0)
    for k in range(steps):
        now, one, two = held.pop(k), held.get(k + 1), held.get(k + 2)
        start = 8 * (k + 3)
        if start < PART:
            below = v_ref[start:, :]
            high, low = halves(below)
            left = jnp.concatenate([high, high, low], axis=1)
            at = lax.broadcasted_iota(jnp.int32, (PART - start, PART), 1)
            keep = jnp.where((at >= 8 * k) & (at < 8 * k + 8), 0.0, below)
        far = columns(two, k) if two is not None else None
        next_pivot = columns(one, k + 1) if one is not None else None
        next_near = columns(two, k + 1) if two is not None else None
        here = (lane >= 8 * k) & (lane < 8 * k + 8)
        now = jnp.where(here, (lane - 8 * k == sub).astype(F32), now)
        if one is not None:
            one = jnp.where(here, 0.0, one)
        if two is not None:
            two = jnp.where(here, 0.0, two)
        scale = jnp.zeros((8, PART), F32)
        unscale = scale
        done = now
        for i in range(8):
            value = spread(pivot[i][i : i + 1])
            inverse = 1.0 / value
            scale = jnp.where(sub == i, value, scale)
            unscale = jnp.where(sub == i, inverse, unscale)
            if i > 0:
                done = jnp.where(sub == i, now, done)
            f0 = jnp.where(sub != i, pivot[i] * inverse, 0.0)
            f1 = near[i] * inverse if one is not None else None
            f2 = far[i] * inverse if two is not None else None
            for c in range(i + 1, 8):
                row = spread(pivot[c][i : i + 1])
                pivot[c] = pivot[c] - f0 * row
                if one is not None:
                    near[c] = near[c] - f1 * row
                if two is not None:
                    far[c] = far[c] - f2 * row
            if one is not None:
                for c in range(8):
                    row = spread(near[i][c : c + 1])
                    next_pivot[c] = next_pivot[c] - f1 * row
                    if two is not None:
                        next_near[c] = next_near[c] - f2 * row
            row = spread(now[i : i + 1])
            now = now - f0 * row
            if one is not None:
                one = one - f1 * row
            if two is not None:
                two = two - f2 * row
        v_ref[8 * k : 8 * k + 8, :] = done * lax.rsqrt(scale)
        if one is not None:
            held[k + 1] = one
        if two is not None:
            held[k + 2] = two
        pivot, near = next_pivot, next_near
        if start < PART:
            rows = [now * unscale, jnp.zeros((PART - 8 - 8 * k, PART), F32)]
            if k > 0:
                rows = [jnp.zeros((8 * k, PART), F32)] + rows
            high, low = halves(jnp.concatenate(rows, axis=0))
            right = jnp.concatenate([high, low, high], axis=0)
            v_ref[start:, :] = keep - dot(left, right, ((1,), (0,)))
            held[k + 3] = rows_at(k + 3)


def tile_of(block):
    return block.reshape(EXAMPLES, TILE)


def layer_anchor(low, high, at, prior_ref):
    inside = (at >= low) & (at < high)
    return jnp.sum(jnp.where(inside, prior_ref[...], 0.0), axis=0, keepdims=True)


def panel_kernel(info_ref, first_ref, index_ref, prior_ref, out_ref, v_ref, *scratch):
    parts = TILE // PART
    r_refs, (t_ref, f_ref, z_ref, made, zero, sems) = scratch[:parts], scratch[parts:]
    lead, place = info_ref[0], info_ref[1]

    def store(source, k):
        return pltpu.make_async_copy(source, out_ref.at[0, k], sems.at[k])

    zero[...] = jnp.zeros((TILE, TILE), F32)
    for k in range(1, BAND):
        @pl.when(k > place)
        def _():
            store(zero, k).start()

    tile = tile_of(first_ref[:, :, :TILE])
    own = tile_of(first_ref[:, :, WIDE:])
    turned_own = own.T
    own2 = jnp.concatenate([turned_own, turned_own], axis=1)
    note = first_ref[pl.ds(lead, 1), :, TILE:WIDE].reshape(2, PART).astype(F32)
    note = 32.0 * note[0:1, :] + note[1:2, :]
    r32 = lax.broadcasted_iota(jnp.int32, (LAYERS, PART), 0)
    c32 = lax.broadcasted_iota(jnp.int32, (LAYERS, PART), 1)
    low = jnp.sum(jnp.where(c32 == r32, note, 0.0), axis=1, keepdims=True)
    high = jnp.sum(jnp.where(c32 == r32 + LAYERS, note, 0.0), axis=1, keepdims=True)
    at = lax.broadcasted_iota(jnp.int32, (LAYERS, TILE), 1).astype(F32)
    anchor = layer_anchor(low, high, at, prior_ref)

    r128 = lax.broadcasted_iota(jnp.int32, (PART, PART), 0)
    c128 = lax.broadcasted_iota(jnp.int32, (PART, PART), 1)
    turned = tile.astype(F32).T
    for b in range(parts):
        block = slice(b * PART, (b + 1) * PART)
        gram = dot(tile[:, block], tile[:, b * PART :], ((0,), (0,)))
        t_ref[b] = gram[:, :PART] + jnp.where(r128 == c128, anchor[:, block], 0.0)
        if b < parts - 1:
            r_refs[b][:, : TILE - (b + 1) * PART] = gram[:, PART:]
        r_refs[b][:, TILE - (b + 1) * PART :] = turned[block, :]

    for b in range(parts):
        block = slice(b * PART, (b + 1) * PART)
        after = (b + 1) * PART
        f_ref[b] = t_ref[b]
        factor_part(f_ref.at[b])
        inverse = jnp.where(c128 <= r128, f_ref[b], 0.0)
        if b < parts - 1:
            first = dot_wide(inverse, r_refs[b][:, :PART], 1)
            t_ref[b + 1] = t_ref[b + 1] - dot_wide(first, first, 0)
            others = dot_wide(inverse, r_refs[b][:, PART:], 1)
            solved = jnp.concatenate([first, others], axis=1)
            for c in range(b + 1, parts):
                skip = (c - b - 1) * PART
                change = dot_wide(solved[:, skip : skip + PART], solved[:, skip:], 0)
                if c > b + 1:
                    t_ref[c] = t_ref[c] - change[:, :PART]
                r_refs[c][...] = r_refs[c][...] - change[:, PART:]
        else:
            solved = dot_wide(inverse, r_refs[b][...], 1)
        zt = solved[:, TILE - after :]
        z_ref[block, :] = zt

    zt = z_ref[...]
    made[1] = dot(own2, jnp.concatenate(halves(zt), axis=1), ((1,), (1,)))

    @pl.when(place == 0)
    def _():
        for b in range(parts):
            block = slice(b * PART, (b + 1) * PART)
            if b > 0:
                made[1, : b * PART, block] = jnp.zeros((b * PART, PART), F32)
            inverse = jnp.where(c128 <= r128, f_ref[b], 0.0)
            th, tl = halves(t_ref[b])
            ih, il = halves(inverse)
            left = jnp.concatenate([th, th, tl], axis=1)
            right = jnp.concatenate([ih, il, ih], axis=1)
            made[1, block, block] = jnp.where(c128 <= r128, dot(left, right, ((1,), (1,))), 0.0)

    store(made.at[1], place).start()
    r256 = lax.broadcasted_iota(jnp.int32, (EXAMPLES, EXAMPLES), 0)
    c256 = lax.broadcasted_iota(jnp.int32, (EXAMPLES, EXAMPLES), 1)
    w = (r256 == c256).astype(F32) - dot_wide(zt, zt, 0)
    w2 = jnp.concatenate(halves(w), axis=0)
    v = jnp.concatenate(halves(dot(own2, w2, ((1,), (0,)))), axis=1)
    v_ref[...] = v

    @pl.when(place > 0)
    def _():
        layer = lax.broadcasted_iota(jnp.int32, (LAYERS, TILE), 0) * SPAN
        own_anchor = layer_anchor(layer, layer + SPAN, index_ref[...], prior_ref)
        row = lax.broadcasted_iota(jnp.int32, (TILE, TILE), 0)
        column = lax.broadcasted_iota(jnp.int32, (TILE, TILE), 1)
        own = tile_of(first_ref[:, :, WIDE:])
        base = dot(v_ref[...], jnp.concatenate([own, own], axis=0), ((1,), (0,)))
        made[0] = base + jnp.where(row == column, own_anchor, 0.0)
        store(made.at[0], 0).start()
        store(made.at[0], 0).wait()

    store(made.at[1], place).wait()
    for k in range(1, BAND):
        @pl.when(k > place)
        def _():
            store(zero, k).wait()


def band_kernel(place_ref, v_ref, rest_ref, moved_ref, before_ref, out_ref, made, sems):
    place = place_ref[0]

    def store(k):
        return pltpu.make_async_copy(made.at[k - 1], out_ref.at[0, k], sems.at[k - 1])

    def fill(k, block):
        other = tile_of(block)
        made[k - 1] = dot(v_ref[...], jnp.concatenate([other, other], axis=0), ((1,), (0,)))
        store(k).start()

    @pl.when(place == BAND - 1)
    def _():
        fill(1, moved_ref[...])

    for k in range(1, BAND - 1):
        @pl.when((k < place) & (place - k < BAND - 2))
        def _():
            start = pl.multiple_of((place - k - 1) * TILE, TILE)
            fill(k, rest_ref[:, :, pl.ds(start, TILE)])

    for k in range(1, BAND - 1):
        @pl.when(k < place)
        def _():
            store(k).wait()


SMEM = pl.BlockSpec(memory_space=pltpu.SMEM)
VMEM = pl.BlockSpec(memory_space=pltpu.VMEM)
HBM = pl.BlockSpec(memory_space=pl.ANY)


def body(jacobian, curvature, sub_index, prior_precision):
    position = lax.axis_index(AXES).astype(jnp.int32)
    place = lax.rem(position, BAND)
    index = sub_index.reshape(1, TILE)
    prior = prior_precision.reshape(LAYERS, 1)
    send_first = pl.pallas_call(
        first_kernel,
        out_shape=pltpu.VMEM((GROUPS, BAND, 2, WIDE + TILE), BF16),
        in_specs=[SMEM, VMEM, VMEM],
        out_specs=VMEM,
        compiler_params=params(),
        name="first_send",
    )(curvature, jacobian, index)
    first = lax.all_to_all(
        send_first.reshape(DEVICES, 2, WIDE + TILE), AXES, split_axis=0, concat_axis=0, tiled=True
    )
    send_rest = pl.pallas_call(
        rest_kernel,
        out_shape=jax.ShapeDtypeStruct((GROUPS, BAND, 2, REST), BF16),
        in_specs=[SMEM, VMEM],
        out_specs=HBM,
        scratch_shapes=[pltpu.VMEM((GROUPS, 2, REST), BF16), pltpu.SemaphoreType.DMA((BAND,))],
        compiler_params=params(),
        name="rest_send",
    )(curvature, jacobian)
    send_rest, first = lax.optimization_barrier((send_rest, first))
    rest = lax.all_to_all(
        send_rest.reshape(DEVICES, 2, REST), AXES, split_axis=0, concat_axis=0, tiled=True
    )
    pairs = [(h * BAND + BAND - 2, h * BAND + BAND - 1) for h in range(2)]
    moved = lax.ppermute(first[:, :, WIDE:], "col", pairs)
    parts = TILE // PART
    before, v = pl.pallas_call(
        panel_kernel,
        out_shape=[
            jax.ShapeDtypeStruct((1, BAND, TILE, TILE), F32),
            pltpu.VMEM((TILE, 2 * EXAMPLES), BF16),
        ],
        in_specs=[SMEM, VMEM, VMEM, VMEM],
        out_specs=[HBM, VMEM],
        scratch_shapes=[pltpu.VMEM((PART, TILE - (b + 1) * PART + EXAMPLES), F32) for b in range(parts)]
        + [
            pltpu.VMEM((parts, PART, PART), F32),
            pltpu.VMEM((parts, PART, PART), F32),
            pltpu.VMEM((TILE, EXAMPLES), F32),
            pltpu.VMEM((2, TILE, TILE), F32),
            pltpu.VMEM((TILE, TILE), F32),
            pltpu.SemaphoreType.DMA((BAND,)),
        ],
        compiler_params=params(),
        cost_estimate=pl.CostEstimate(flops=2 * 10**10, bytes_accessed=2 * 10**6, transcendentals=10**6),
        name="panel",
    )(jnp.stack([position - place, place]), pltpu.with_memory_space_constraint(first, pltpu.VMEM), index, prior)
    return pl.pallas_call(
        band_kernel,
        out_shape=jax.ShapeDtypeStruct((1, BAND, TILE, TILE), F32),
        in_specs=[SMEM, VMEM, VMEM, VMEM, HBM],
        out_specs=HBM,
        scratch_shapes=[
            pltpu.VMEM((BAND - 2, TILE, TILE), F32),
            pltpu.SemaphoreType.DMA((BAND - 2,)),
        ],
        input_output_aliases={4: 0},
        compiler_params=params(),
        name="band",
    )(place.reshape(1), pltpu.with_memory_space_constraint(v, pltpu.VMEM), pltpu.with_memory_space_constraint(rest, pltpu.VMEM), pltpu.with_memory_space_constraint(moved, pltpu.VMEM), before)


def solution(mesh):
    placed = (P(AXES, None), P(AXES), P(AXES), P())
    return jax.shard_map(
        body,
        mesh=mesh,
        in_specs=placed,
        out_specs=P(AXES, None, None, None),
        check_vma=False,
    )
```

```python
import jax
import jax.numpy as jnp
from jax import lax
from jax.experimental import pallas as pl
from jax.experimental.pallas import tpu as pltpu
from jax.sharding import PartitionSpec as P

TILE = 512
BAND = 8
LAYERS = 32
SPAN = 131072
GROUPS = 16
DEVICES = 128
EXAMPLES = 256
WIDE = TILE + 128
SENT = 5
REST = SENT * TILE
STEPS = BAND - 2 - SENT
PART = 128
F32 = jnp.float32
BF16 = jnp.bfloat16
AXES = ("row", "col")
VMEM_LIMIT = 56 * 1024 * 1024


def params():
    return pltpu.CompilerParams(vmem_limit_bytes=VMEM_LIMIT)


def halves(x):
    high = x.astype(BF16)
    return high, (x - high.astype(F32)).astype(BF16)


def dot(a, b, contract):
    return lax.dot_general(a, b, ((contract[0], contract[1]), ((), ())), preferred_element_type=F32)


def dot_wide(a, b, axis):
    ah, al = halves(a)
    bh, bl = halves(b)
    left = jnp.concatenate([ah, ah, al], axis=axis)
    right = jnp.concatenate([bh, bl, bh], axis=0)
    return dot(left, right, ((axis,), (0,)))


def root_curvature(curvature_ref, width):
    rows = lax.broadcasted_iota(jnp.int32, (2, width), 0)
    return jnp.sqrt(jnp.where(rows == 0, curvature_ref[0], curvature_ref[1]))


def first_kernel(curvature_ref, jacobian_ref, index_ref, out_ref):
    root = root_curvature(curvature_ref, BAND * TILE)
    slot = lax.broadcasted_iota(jnp.int32, (PART, TILE), 0)
    layer = jnp.where(slot < LAYERS, slot, slot - (LAYERS - 1))
    below = (index_ref[...] < layer * SPAN).astype(F32)
    counts = jnp.sum(below, axis=1, keepdims=True)
    eye = lax.broadcasted_iota(jnp.int32, (PART, PART), 0) == lax.broadcasted_iota(jnp.int32, (PART, PART), 1)
    counts = jnp.sum(jnp.where(eye, counts, 0.0), axis=0, keepdims=True)
    high = jnp.floor(counts * (1.0 / 32.0))
    low = counts - 32.0 * high
    rows = lax.broadcasted_iota(jnp.int32, (2, PART), 0)
    tail = jnp.where(rows == 0, high, low).astype(BF16)
    for g in range(GROUPS):
        block = jacobian_ref[:, g * BAND * TILE : (g + 1) * BAND * TILE].astype(F32)
        block = (root * block).astype(BF16)
        for i in range(BAND):
            out_ref[g, i, :, :TILE] = block[:, :TILE]
            out_ref[g, i, :, TILE:WIDE] = tail
            out_ref[g, i, :, WIDE:] = block[:, i * TILE : (i + 1) * TILE]


def rest_kernel(curvature_ref, jacobian_ref, out_ref, held, sems):
    root = root_curvature(curvature_ref, REST)
    for g in range(GROUPS):
        start = g * BAND * TILE + TILE
        block = jacobian_ref[:, start : start + REST].astype(F32)
        held[g] = (root * block).astype(BF16)
    copies = [pltpu.make_async_copy(held, out_ref.at[:, i], sems.at[i]) for i in range(BAND)]
    for copy in copies:
        copy.start()
    for copy in copies:
        copy.wait()


def factor_part(v_ref):
    sub = lax.broadcasted_iota(jnp.int32, (8, PART), 0)
    lane = lax.broadcasted_iota(jnp.int32, (8, PART), 1)
    steps = PART // 8

    def spread(x):
        return jnp.broadcast_to(x, (8, PART))

    def rows_at(k):
        return v_ref[8 * k : 8 * k + 8, :]

    def columns(x, k):
        return [spread(x[:, 8 * k + c : 8 * k + c + 1]) for c in range(8)]

    held = {k: rows_at(k) for k in range(3)}
    pivot = columns(held[0], 0)
    near = columns(held[1], 0)
    for k in range(steps):
        now, one, two = held.pop(k), held.get(k + 1), held.get(k + 2)
        start = 8 * (k + 3)
        if start < PART:
            below = v_ref[start:, :]
            high, low = halves(below)
            left = jnp.concatenate([high, high, low], axis=1)
            at = lax.broadcasted_iota(jnp.int32, (PART - start, PART), 1)
            keep = jnp.where((at >= 8 * k) & (at < 8 * k + 8), 0.0, below)
        far = columns(two, k) if two is not None else None
        next_pivot = columns(one, k + 1) if one is not None else None
        next_near = columns(two, k + 1) if two is not None else None
        here = (lane >= 8 * k) & (lane < 8 * k + 8)
        now = jnp.where(here, (lane - 8 * k == sub).astype(F32), now)
        if one is not None:
            one = jnp.where(here, 0.0, one)
        if two is not None:
            two = jnp.where(here, 0.0, two)
        scale = jnp.zeros((8, PART), F32)
        unscale = scale
        done = now
        for i in range(8):
            value = spread(pivot[i][i : i + 1])
            inverse = 1.0 / value
            scale = jnp.where(sub == i, value, scale)
            unscale = jnp.where(sub == i, inverse, unscale)
            if i > 0:
                done = jnp.where(sub == i, now, done)
            f0 = jnp.where(sub != i, pivot[i] * inverse, 0.0)
            f1 = near[i] * inverse if one is not None else None
            f2 = far[i] * inverse if two is not None else None
            for c in range(i + 1, 8):
                row = spread(pivot[c][i : i + 1])
                pivot[c] = pivot[c] - f0 * row
                if one is not None:
                    near[c] = near[c] - f1 * row
                if two is not None:
                    far[c] = far[c] - f2 * row
            if one is not None:
                for c in range(8):
                    row = spread(near[i][c : c + 1])
                    next_pivot[c] = next_pivot[c] - f1 * row
                    if two is not None:
                        next_near[c] = next_near[c] - f2 * row
            row = spread(now[i : i + 1])
            now = now - f0 * row
            if one is not None:
                one = one - f1 * row
            if two is not None:
                two = two - f2 * row
        v_ref[8 * k : 8 * k + 8, :] = done * lax.rsqrt(scale)
        if one is not None:
            held[k + 1] = one
        if two is not None:
            held[k + 2] = two
        pivot, near = next_pivot, next_near
        if start < PART:
            rows = [now * unscale, jnp.zeros((PART - 8 - 8 * k, PART), F32)]
            if k > 0:
                rows = [jnp.zeros((8 * k, PART), F32)] + rows
            high, low = halves(jnp.concatenate(rows, axis=0))
            right = jnp.concatenate([high, low, high], axis=0)
            v_ref[start:, :] = keep - dot(left, right, ((1,), (0,)))
            held[k + 3] = rows_at(k + 3)


def tile_of(block):
    return block.reshape(EXAMPLES, TILE)


def layer_anchor(low, high, at, prior_ref):
    row = lax.broadcasted_iota(jnp.int32, (LAYERS, LAYERS), 0)
    column = lax.broadcasted_iota(jnp.int32, (LAYERS, LAYERS), 1)
    prior = jnp.sum(jnp.where(row == column, prior_ref[...], 0.0), axis=1, keepdims=True)
    inside = (at >= low) & (at < high)
    return jnp.sum(jnp.where(inside, prior, 0.0), axis=0, keepdims=True)


def panel_kernel(position_ref, first_ref, index_ref, prior_ref, out_ref, v_ref, *scratch):
    parts = TILE // PART
    r_refs, (t_ref, f_ref, z_ref, made, zero, sems) = scratch[:parts], scratch[parts:]
    place = lax.rem(position_ref[0], BAND)
    lead = position_ref[0] - place

    def store(source, k):
        return pltpu.make_async_copy(source, out_ref.at[0, k], sems.at[k])

    zero[...] = jnp.zeros((TILE, TILE), F32)
    for k in range(1, BAND):
        @pl.when(k > place)
        def _():
            store(zero, k).start()

    tile = tile_of(first_ref[:, :, :TILE])
    own = tile_of(first_ref[:, :, WIDE:])
    turned_own = own.T
    own2 = jnp.concatenate([turned_own, turned_own], axis=1)
    note = first_ref[pl.ds(lead, 1), :, TILE:WIDE].reshape(2, PART).astype(F32)
    note = 32.0 * note[0:1, :] + note[1:2, :]
    r32 = lax.broadcasted_iota(jnp.int32, (LAYERS, PART), 0)
    c32 = lax.broadcasted_iota(jnp.int32, (LAYERS, PART), 1)
    low = jnp.sum(jnp.where(c32 == r32, note, 0.0), axis=1, keepdims=True)
    high = jnp.sum(jnp.where(c32 == r32 + LAYERS, note, 0.0), axis=1, keepdims=True)
    at = lax.broadcasted_iota(jnp.int32, (LAYERS, TILE), 1).astype(F32)
    anchor = layer_anchor(low, high, at, prior_ref)

    r128 = lax.broadcasted_iota(jnp.int32, (PART, PART), 0)
    c128 = lax.broadcasted_iota(jnp.int32, (PART, PART), 1)
    turned = tile.astype(F32).T
    for b in range(parts):
        block = slice(b * PART, (b + 1) * PART)
        gram = dot(tile[:, block], tile[:, b * PART :], ((0,), (0,)))
        t_ref[b] = gram[:, :PART] + jnp.where(r128 == c128, anchor[:, block], 0.0)
        if b < parts - 1:
            r_refs[b][:, : TILE - (b + 1) * PART] = gram[:, PART:]
        r_refs[b][:, TILE - (b + 1) * PART :] = turned[block, :]

    for b in range(parts):
        block = slice(b * PART, (b + 1) * PART)
        after = (b + 1) * PART
        f_ref[b] = t_ref[b]
        factor_part(f_ref.at[b])
        inverse = jnp.where(c128 <= r128, f_ref[b], 0.0)
        if b < parts - 1:
            first = dot_wide(inverse, r_refs[b][:, :PART], 1)
            t_ref[b + 1] = t_ref[b + 1] - dot_wide(first, first, 0)
            others = dot_wide(inverse, r_refs[b][:, PART:], 1)
            solved = jnp.concatenate([first, others], axis=1)
            for c in range(b + 1, parts):
                skip = (c - b - 1) * PART
                change = dot_wide(solved[:, skip : skip + PART], solved[:, skip:], 0)
                if c > b + 1:
                    t_ref[c] = t_ref[c] - change[:, :PART]
                r_refs[c][...] = r_refs[c][...] - change[:, PART:]
        else:
            solved = dot_wide(inverse, r_refs[b][...], 1)
        zt = solved[:, TILE - after :]
        z_ref[block, :] = zt

    zt = z_ref[...]
    made[1] = dot(own2, jnp.concatenate(halves(zt), axis=1), ((1,), (1,)))

    @pl.when(place == 0)
    def _():
        for b in range(parts):
            block = slice(b * PART, (b + 1) * PART)
            if b > 0:
                made[1, : b * PART, block] = jnp.zeros((b * PART, PART), F32)
            inverse = jnp.where(c128 <= r128, f_ref[b], 0.0)
            th, tl = halves(t_ref[b])
            ih, il = halves(inverse)
            left = jnp.concatenate([th, th, tl], axis=1)
            right = jnp.concatenate([ih, il, ih], axis=1)
            made[1, block, block] = jnp.where(c128 <= r128, dot(left, right, ((1,), (1,))), 0.0)

    store(made.at[1], place).start()
    r256 = lax.broadcasted_iota(jnp.int32, (EXAMPLES, EXAMPLES), 0)
    c256 = lax.broadcasted_iota(jnp.int32, (EXAMPLES, EXAMPLES), 1)
    w = (r256 == c256).astype(F32) - dot_wide(zt, zt, 0)
    w2 = jnp.concatenate(halves(w), axis=0)
    v = jnp.concatenate(halves(dot(own2, w2, ((1,), (0,)))), axis=1)
    v_ref[...] = v

    @pl.when(place > 0)
    def _():
        layer = lax.broadcasted_iota(jnp.int32, (LAYERS, TILE), 0) * SPAN
        own_anchor = layer_anchor(layer, layer + SPAN, index_ref[...], prior_ref)
        row = lax.broadcasted_iota(jnp.int32, (TILE, TILE), 0)
        column = lax.broadcasted_iota(jnp.int32, (TILE, TILE), 1)
        own = tile_of(first_ref[:, :, WIDE:])
        base = dot(v_ref[...], jnp.concatenate([own, own], axis=0), ((1,), (0,)))
        made[0] = base + jnp.where(row == column, own_anchor, 0.0)
        store(made.at[0], 0).start()
        store(made.at[0], 0).wait()

    store(made.at[1], place).wait()
    for k in range(1, BAND):
        @pl.when(k > place)
        def _():
            store(zero, k).wait()


def write_slots(v_ref, out_ref, made, sems, cases):
    def store(n, k):
        return pltpu.make_async_copy(made.at[n], out_ref.at[0, k], sems.at[n])

    for n, (k, wanted, block) in enumerate(cases):
        @pl.when(wanted)
        def _():
            other = tile_of(block())
            made[n] = dot(v_ref[...], jnp.concatenate([other, other], axis=0), ((1,), (0,)))
            store(n, k).start()

    for n, (k, wanted, block) in enumerate(cases):
        @pl.when(wanted)
        def _():
            store(n, k).wait()


def band_kernel(position_ref, v_ref, rest_ref, before_ref, out_ref, made, sems):
    place = lax.rem(position_ref[0], BAND)

    def block(k):
        start = pl.multiple_of((place - k - 1) * TILE, TILE)
        return lambda: rest_ref[:, :, pl.ds(start, TILE)]

    cases = [(k, (k < place) & (place - k <= SENT), block(k)) for k in range(1, BAND - 1)]
    write_slots(v_ref, out_ref, made, sems, cases)


def moved_kernel(position_ref, v_ref, before_ref, *rest):
    moved, (out_ref, made, sems) = rest[:STEPS], rest[STEPS:]
    place = lax.rem(position_ref[0], BAND)
    cases = [(k, place - k > SENT, lambda k=k: moved[k - 1][...]) for k in range(1, STEPS + 1)]
    write_slots(v_ref, out_ref, made, sems, cases)


def close(x):
    return pltpu.with_memory_space_constraint(x, pltpu.VMEM)


SMEM = pl.BlockSpec(memory_space=pltpu.SMEM)
VMEM = pl.BlockSpec(memory_space=pltpu.VMEM)
HBM = pl.BlockSpec(memory_space=pl.ANY)


def body(jacobian, curvature, sub_index, prior_precision):
    position = lax.axis_index(AXES).astype(jnp.int32)
    index = sub_index.reshape(1, TILE)
    prior = prior_precision.reshape(1, LAYERS)
    send_first = pl.pallas_call(
        first_kernel,
        out_shape=pltpu.VMEM((GROUPS, BAND, 2, WIDE + TILE), BF16),
        in_specs=[SMEM, VMEM, VMEM],
        out_specs=VMEM,
        compiler_params=params(),
        name="first_send",
    )(curvature, jacobian, index)
    first = lax.all_to_all(
        send_first.reshape(DEVICES, 2, WIDE + TILE), AXES, split_axis=0, concat_axis=0, tiled=True
    )
    send_rest = pl.pallas_call(
        rest_kernel,
        out_shape=jax.ShapeDtypeStruct((GROUPS, BAND, 2, REST), BF16),
        in_specs=[SMEM, VMEM],
        out_specs=HBM,
        scratch_shapes=[pltpu.VMEM((GROUPS, 2, REST), BF16), pltpu.SemaphoreType.DMA((BAND,))],
        compiler_params=params(),
        name="rest_send",
    )(curvature, jacobian)
    send_rest, first = lax.optimization_barrier((send_rest, first))
    rest = lax.all_to_all(
        send_rest.reshape(DEVICES, 2, REST), AXES, split_axis=0, concat_axis=0, tiled=True
    )
    moved = []
    for step in range(STEPS, 0, -1):
        pairs = [
            (h * BAND + i, h * BAND + i + step) for h in range(2) for i in range(SENT + 1, BAND - step)
        ]
        moved.insert(0, lax.ppermute(first[:, :, WIDE:], "col", pairs))
    parts = TILE // PART
    before, v = pl.pallas_call(
        panel_kernel,
        out_shape=[
            jax.ShapeDtypeStruct((1, BAND, TILE, TILE), F32),
            pltpu.VMEM((TILE, 2 * EXAMPLES), BF16),
        ],
        in_specs=[SMEM, VMEM, VMEM, VMEM],
        out_specs=[HBM, VMEM],
        scratch_shapes=[pltpu.VMEM((PART, TILE - (b + 1) * PART + EXAMPLES), F32) for b in range(parts)]
        + [
            pltpu.VMEM((parts, PART, PART), F32),
            pltpu.VMEM((parts, PART, PART), F32),
            pltpu.VMEM((TILE, EXAMPLES), F32),
            pltpu.VMEM((2, TILE, TILE), F32),
            pltpu.VMEM((TILE, TILE), F32),
            pltpu.SemaphoreType.DMA((BAND,)),
        ],
        compiler_params=params(),
        cost_estimate=pl.CostEstimate(flops=2 * 10**9, bytes_accessed=2 * 10**6, transcendentals=10**6),
        name="panel",
    )(position.reshape(1), pltpu.with_memory_space_constraint(first, pltpu.VMEM), index, prior)
    slots = jax.ShapeDtypeStruct((1, BAND, TILE, TILE), F32)
    before = pl.pallas_call(
        band_kernel,
        out_shape=slots,
        in_specs=[SMEM, VMEM, VMEM, HBM],
        out_specs=HBM,
        scratch_shapes=[pltpu.VMEM((BAND - 2, TILE, TILE), F32), pltpu.SemaphoreType.DMA((BAND - 2,))],
        input_output_aliases={3: 0},
        compiler_params=params(),
        name="band",
    )(position.reshape(1), close(v), close(rest), before)
    return pl.pallas_call(
        moved_kernel,
        out_shape=slots,
        in_specs=[SMEM, VMEM, HBM] + [VMEM] * STEPS,
        out_specs=HBM,
        scratch_shapes=[pltpu.VMEM((STEPS, TILE, TILE), F32), pltpu.SemaphoreType.DMA((STEPS,))],
        input_output_aliases={2: 0},
        compiler_params=params(),
        name="moved",
    )(position.reshape(1), close(v), before, *[close(x) for x in moved])


def solution(mesh):
    placed = (P(AXES, None), P(AXES), P(AXES), P())
    return jax.shard_map(
        body,
        mesh=mesh,
        in_specs=placed,
        out_specs=P(AXES, None, None, None),
        check_vma=False,
    )
```

```python
import jax
import jax.numpy as jnp
from jax import lax
from jax.experimental import pallas as pl
from jax.experimental.pallas import tpu as pltpu
from jax.sharding import PartitionSpec as P

TILE = 512
BAND = 8
LAYERS = 32
SPAN = 131072
GROUPS = 16
DEVICES = 128
EXAMPLES = 256
WIDE = TILE + 128
SENT = 4
REST = SENT * TILE
STEPS = BAND - 2 - SENT
PART = 128
F32 = jnp.float32
BF16 = jnp.bfloat16
AXES = ("row", "col")
VMEM_LIMIT = 56 * 1024 * 1024


def params():
    return pltpu.CompilerParams(vmem_limit_bytes=VMEM_LIMIT)


def halves(x):
    high = x.astype(BF16)
    return high, (x - high.astype(F32)).astype(BF16)


def dot(a, b, contract):
    return lax.dot_general(a, b, ((contract[0], contract[1]), ((), ())), preferred_element_type=F32)


def dot_wide(a, b, axis):
    ah, al = halves(a)
    bh, bl = halves(b)
    left = jnp.concatenate([ah, ah, al], axis=axis)
    right = jnp.concatenate([bh, bl, bh], axis=0)
    return dot(left, right, ((axis,), (0,)))


def root_curvature(curvature_ref, width):
    rows = lax.broadcasted_iota(jnp.int32, (2, width), 0)
    return jnp.sqrt(jnp.where(rows == 0, curvature_ref[0], curvature_ref[1]))


def first_kernel(curvature_ref, jacobian_ref, index_ref, out_ref):
    root = root_curvature(curvature_ref, BAND * TILE)
    slot = lax.broadcasted_iota(jnp.int32, (PART, TILE), 0)
    layer = jnp.where(slot < LAYERS, slot, slot - (LAYERS - 1))
    below = (index_ref[...] < layer * SPAN).astype(F32)
    counts = jnp.sum(below, axis=1, keepdims=True)
    eye = lax.broadcasted_iota(jnp.int32, (PART, PART), 0) == lax.broadcasted_iota(jnp.int32, (PART, PART), 1)
    counts = jnp.sum(jnp.where(eye, counts, 0.0), axis=0, keepdims=True)
    high = jnp.floor(counts * (1.0 / 32.0))
    low = counts - 32.0 * high
    rows = lax.broadcasted_iota(jnp.int32, (2, PART), 0)
    tail = jnp.where(rows == 0, high, low).astype(BF16)
    for g in range(GROUPS):
        block = jacobian_ref[:, g * BAND * TILE : (g + 1) * BAND * TILE].astype(F32)
        block = (root * block).astype(BF16)
        for i in range(BAND):
            out_ref[g, i, :, :TILE] = block[:, :TILE]
            out_ref[g, i, :, TILE:WIDE] = tail
            out_ref[g, i, :, WIDE:] = block[:, i * TILE : (i + 1) * TILE]


def rest_kernel(curvature_ref, jacobian_ref, out_ref, held, sems):
    root = root_curvature(curvature_ref, REST)
    for g in range(GROUPS):
        start = g * BAND * TILE + TILE
        block = jacobian_ref[:, start : start + REST].astype(F32)
        held[g] = (root * block).astype(BF16)
    copies = [pltpu.make_async_copy(held, out_ref.at[:, i], sems.at[i]) for i in range(BAND)]
    for copy in copies:
        copy.start()
    for copy in copies:
        copy.wait()


def factor_part(v_ref):
    sub = lax.broadcasted_iota(jnp.int32, (8, PART), 0)
    lane = lax.broadcasted_iota(jnp.int32, (8, PART), 1)
    steps = PART // 8

    def spread(x):
        return jnp.broadcast_to(x, (8, PART))

    def rows_at(k):
        return v_ref[8 * k : 8 * k + 8, :]

    def columns(x, k):
        return [spread(x[:, 8 * k + c : 8 * k + c + 1]) for c in range(8)]

    held = {k: rows_at(k) for k in range(3)}
    pivot = columns(held[0], 0)
    near = columns(held[1], 0)
    for k in range(steps):
        now, one, two = held.pop(k), held.get(k + 1), held.get(k + 2)
        start = 8 * (k + 3)
        if start < PART:
            below = v_ref[start:, :]
            high, low = halves(below)
            left = jnp.concatenate([high, high, low], axis=1)
            at = lax.broadcasted_iota(jnp.int32, (PART - start, PART), 1)
            keep = jnp.where((at >= 8 * k) & (at < 8 * k + 8), 0.0, below)
        far = columns(two, k) if two is not None else None
        next_pivot = columns(one, k + 1) if one is not None else None
        next_near = columns(two, k + 1) if two is not None else None
        here = (lane >= 8 * k) & (lane < 8 * k + 8)
        now = jnp.where(here, (lane - 8 * k == sub).astype(F32), now)
        if one is not None:
            one = jnp.where(here, 0.0, one)
        if two is not None:
            two = jnp.where(here, 0.0, two)
        scale = jnp.zeros((8, PART), F32)
        unscale = scale
        done = now
        for i in range(8):
            value = spread(pivot[i][i : i + 1])
            inverse = 1.0 / value
            scale = jnp.where(sub == i, value, scale)
            unscale = jnp.where(sub == i, inverse, unscale)
            if i > 0:
                done = jnp.where(sub == i, now, done)
            f0 = jnp.where(sub != i, pivot[i] * inverse, 0.0)
            f1 = near[i] * inverse if one is not None else None
            f2 = far[i] * inverse if two is not None else None
            for c in range(i + 1, 8):
                row = spread(pivot[c][i : i + 1])
                pivot[c] = pivot[c] - f0 * row
                if one is not None:
                    near[c] = near[c] - f1 * row
                if two is not None:
                    far[c] = far[c] - f2 * row
            if one is not None:
                for c in range(8):
                    row = spread(near[i][c : c + 1])
                    next_pivot[c] = next_pivot[c] - f1 * row
                    if two is not None:
                        next_near[c] = next_near[c] - f2 * row
            row = spread(now[i : i + 1])
            now = now - f0 * row
            if one is not None:
                one = one - f1 * row
            if two is not None:
                two = two - f2 * row
        v_ref[8 * k : 8 * k + 8, :] = done * lax.rsqrt(scale)
        if one is not None:
            held[k + 1] = one
        if two is not None:
            held[k + 2] = two
        pivot, near = next_pivot, next_near
        if start < PART:
            rows = [now * unscale, jnp.zeros((PART - 8 - 8 * k, PART), F32)]
            if k > 0:
                rows = [jnp.zeros((8 * k, PART), F32)] + rows
            high, low = halves(jnp.concatenate(rows, axis=0))
            right = jnp.concatenate([high, low, high], axis=0)
            v_ref[start:, :] = keep - dot(left, right, ((1,), (0,)))
            held[k + 3] = rows_at(k + 3)


def tile_of(block):
    return block.reshape(EXAMPLES, TILE)


def layer_anchor(low, high, at, prior_ref):
    row = lax.broadcasted_iota(jnp.int32, (LAYERS, LAYERS), 0)
    column = lax.broadcasted_iota(jnp.int32, (LAYERS, LAYERS), 1)
    prior = jnp.sum(jnp.where(row == column, prior_ref[...], 0.0), axis=1, keepdims=True)
    inside = (at >= low) & (at < high)
    return jnp.sum(jnp.where(inside, prior, 0.0), axis=0, keepdims=True)


def panel_kernel(position_ref, first_ref, index_ref, prior_ref, out_ref, v_ref, *scratch):
    parts = TILE // PART
    r_refs, (t_ref, f_ref, z_ref, made, zero, sems) = scratch[:parts], scratch[parts:]
    place = lax.rem(position_ref[0], BAND)
    lead = position_ref[0] - place

    def store(source, k):
        return pltpu.make_async_copy(source, out_ref.at[0, k], sems.at[k])

    zero[...] = jnp.zeros((TILE, TILE), F32)
    for k in range(1, BAND):
        @pl.when(k > place)
        def _():
            store(zero, k).start()

    tile = tile_of(first_ref[:, :, :TILE])
    own = tile_of(first_ref[:, :, WIDE:])
    turned_own = own.T
    own2 = jnp.concatenate([turned_own, turned_own], axis=1)
    note = first_ref[pl.ds(lead, 1), :, TILE:WIDE].reshape(2, PART).astype(F32)
    note = 32.0 * note[0:1, :] + note[1:2, :]
    r32 = lax.broadcasted_iota(jnp.int32, (LAYERS, PART), 0)
    c32 = lax.broadcasted_iota(jnp.int32, (LAYERS, PART), 1)
    low = jnp.sum(jnp.where(c32 == r32, note, 0.0), axis=1, keepdims=True)
    high = jnp.sum(jnp.where(c32 == r32 + LAYERS, note, 0.0), axis=1, keepdims=True)
    at = lax.broadcasted_iota(jnp.int32, (LAYERS, TILE), 1).astype(F32)
    anchor = layer_anchor(low, high, at, prior_ref)

    r128 = lax.broadcasted_iota(jnp.int32, (PART, PART), 0)
    c128 = lax.broadcasted_iota(jnp.int32, (PART, PART), 1)
    turned = tile.astype(F32).T
    for b in range(parts):
        block = slice(b * PART, (b + 1) * PART)
        gram = dot(tile[:, block], tile[:, b * PART :], ((0,), (0,)))
        t_ref[b] = gram[:, :PART] + jnp.where(r128 == c128, anchor[:, block], 0.0)
        if b < parts - 1:
            r_refs[b][:, : TILE - (b + 1) * PART] = gram[:, PART:]
        r_refs[b][:, TILE - (b + 1) * PART :] = turned[block, :]

    for b in range(parts):
        block = slice(b * PART, (b + 1) * PART)
        after = (b + 1) * PART
        f_ref[b] = t_ref[b]
        factor_part(f_ref.at[b])
        inverse = jnp.where(c128 <= r128, f_ref[b], 0.0)
        if b < parts - 1:
            first = dot_wide(inverse, r_refs[b][:, :PART], 1)
            t_ref[b + 1] = t_ref[b + 1] - dot_wide(first, first, 0)
            others = dot_wide(inverse, r_refs[b][:, PART:], 1)
            solved = jnp.concatenate([first, others], axis=1)
            for c in range(b + 1, parts):
                skip = (c - b - 1) * PART
                change = dot_wide(solved[:, skip : skip + PART], solved[:, skip:], 0)
                if c > b + 1:
                    t_ref[c] = t_ref[c] - change[:, :PART]
                r_refs[c][...] = r_refs[c][...] - change[:, PART:]
        else:
            solved = dot_wide(inverse, r_refs[b][...], 1)
        zt = solved[:, TILE - after :]
        z_ref[block, :] = zt

    zt = z_ref[...]
    made[1] = dot(own2, jnp.concatenate(halves(zt), axis=1), ((1,), (1,)))

    @pl.when(place == 0)
    def _():
        for b in range(parts):
            block = slice(b * PART, (b + 1) * PART)
            if b > 0:
                made[1, : b * PART, block] = jnp.zeros((b * PART, PART), F32)
            inverse = jnp.where(c128 <= r128, f_ref[b], 0.0)
            th, tl = halves(t_ref[b])
            ih, il = halves(inverse)
            left = jnp.concatenate([th, th, tl], axis=1)
            right = jnp.concatenate([ih, il, ih], axis=1)
            made[1, block, block] = jnp.where(c128 <= r128, dot(left, right, ((1,), (1,))), 0.0)

    store(made.at[1], place).start()
    r256 = lax.broadcasted_iota(jnp.int32, (EXAMPLES, EXAMPLES), 0)
    c256 = lax.broadcasted_iota(jnp.int32, (EXAMPLES, EXAMPLES), 1)
    w = (r256 == c256).astype(F32) - dot_wide(zt, zt, 0)
    w2 = jnp.concatenate(halves(w), axis=0)
    v = jnp.concatenate(halves(dot(own2, w2, ((1,), (0,)))), axis=1)
    v_ref[...] = v

    @pl.when(place > 0)
    def _():
        layer = lax.broadcasted_iota(jnp.int32, (LAYERS, TILE), 0) * SPAN
        own_anchor = layer_anchor(layer, layer + SPAN, index_ref[...], prior_ref)
        row = lax.broadcasted_iota(jnp.int32, (TILE, TILE), 0)
        column = lax.broadcasted_iota(jnp.int32, (TILE, TILE), 1)
        own = tile_of(first_ref[:, :, WIDE:])
        base = dot(v_ref[...], jnp.concatenate([own, own], axis=0), ((1,), (0,)))
        made[0] = base + jnp.where(row == column, own_anchor, 0.0)
        store(made.at[0], 0).start()
        store(made.at[0], 0).wait()

    store(made.at[1], place).wait()
    for k in range(1, BAND):
        @pl.when(k > place)
        def _():
            store(zero, k).wait()


def write_slots(v_ref, out_ref, made, sems, cases):
    half = TILE // 2

    def store(n, k, part):
        rows = pl.ds(part * half, half)
        return pltpu.make_async_copy(made.at[n, rows], out_ref.at[0, k, rows], sems.at[n, part])

    for n, (k, wanted, block) in enumerate(cases):
        @pl.when(wanted)
        def _():
            other = tile_of(block())
            pair = jnp.concatenate([other, other], axis=0)
            for part in range(2):
                rows = slice(part * half, (part + 1) * half)
                made[n, rows] = dot(v_ref[rows, :], pair, ((1,), (0,)))
                store(n, k, part).start()

    for n, (k, wanted, block) in enumerate(cases):
        @pl.when(wanted)
        def _():
            for part in range(2):
                store(n, k, part).wait()


def band_kernel(position_ref, v_ref, rest_ref, before_ref, out_ref, made, sems):
    place = lax.rem(position_ref[0], BAND)

    def block(k):
        start = pl.multiple_of((place - k - 1) * TILE, TILE)
        return lambda: rest_ref[:, :, pl.ds(start, TILE)]

    cases = [(k, (k < place) & (place - k <= SENT), block(k)) for k in range(1, BAND - 1)]
    write_slots(v_ref, out_ref, made, sems, cases)


def moved_kernel(position_ref, v_ref, before_ref, *rest):
    moved, (out_ref, made, sems) = rest[:STEPS], rest[STEPS:]
    place = lax.rem(position_ref[0], BAND)
    cases = [(k, place - k > SENT, lambda k=k: moved[k - 1][...]) for k in range(1, STEPS + 1)]
    write_slots(v_ref, out_ref, made, sems, cases)


def close(x):
    return pltpu.with_memory_space_constraint(x, pltpu.VMEM)


SMEM = pl.BlockSpec(memory_space=pltpu.SMEM)
VMEM = pl.BlockSpec(memory_space=pltpu.VMEM)
HBM = pl.BlockSpec(memory_space=pl.ANY)


def body(jacobian, curvature, sub_index, prior_precision):
    position = lax.axis_index(AXES).astype(jnp.int32)
    index = sub_index.reshape(1, TILE)
    prior = prior_precision.reshape(1, LAYERS)
    send_first = pl.pallas_call(
        first_kernel,
        out_shape=pltpu.VMEM((GROUPS, BAND, 2, WIDE + TILE), BF16),
        in_specs=[SMEM, VMEM, VMEM],
        out_specs=VMEM,
        compiler_params=params(),
        name="first_send",
    )(curvature, jacobian, index)
    first = lax.all_to_all(
        send_first.reshape(DEVICES, 2, WIDE + TILE), AXES, split_axis=0, concat_axis=0, tiled=True
    )
    send_rest = pl.pallas_call(
        rest_kernel,
        out_shape=jax.ShapeDtypeStruct((GROUPS, BAND, 2, REST), BF16),
        in_specs=[SMEM, VMEM],
        out_specs=HBM,
        scratch_shapes=[pltpu.VMEM((GROUPS, 2, REST), BF16), pltpu.SemaphoreType.DMA((BAND,))],
        compiler_params=params(),
        name="rest_send",
    )(curvature, jacobian)
    send_rest, first = lax.optimization_barrier((send_rest, first))
    rest = lax.all_to_all(
        send_rest.reshape(DEVICES, 2, REST), AXES, split_axis=0, concat_axis=0, tiled=True
    )
    moved = []
    for step in range(STEPS, 0, -1):
        pairs = [
            (h * BAND + i, h * BAND + i + step) for h in range(2) for i in range(SENT + 1, BAND - step)
        ]
        moved.insert(0, lax.ppermute(first[:, :, WIDE:], "col", pairs))
    parts = TILE // PART
    before, v = pl.pallas_call(
        panel_kernel,
        out_shape=[
            jax.ShapeDtypeStruct((1, BAND, TILE, TILE), F32),
            pltpu.VMEM((TILE, 2 * EXAMPLES), BF16),
        ],
        in_specs=[SMEM, VMEM, VMEM, VMEM],
        out_specs=[HBM, VMEM],
        scratch_shapes=[pltpu.VMEM((PART, TILE - (b + 1) * PART + EXAMPLES), F32) for b in range(parts)]
        + [
            pltpu.VMEM((parts, PART, PART), F32),
            pltpu.VMEM((parts, PART, PART), F32),
            pltpu.VMEM((TILE, EXAMPLES), F32),
            pltpu.VMEM((2, TILE, TILE), F32),
            pltpu.VMEM((TILE, TILE), F32),
            pltpu.SemaphoreType.DMA((BAND,)),
        ],
        compiler_params=params(),
        cost_estimate=pl.CostEstimate(flops=2 * 10**9, bytes_accessed=2 * 10**6, transcendentals=10**6),
        name="panel",
    )(position.reshape(1), pltpu.with_memory_space_constraint(first, pltpu.VMEM), index, prior)
    slots = jax.ShapeDtypeStruct((1, BAND, TILE, TILE), F32)
    before = pl.pallas_call(
        band_kernel,
        out_shape=slots,
        in_specs=[SMEM, VMEM, VMEM, HBM],
        out_specs=HBM,
        scratch_shapes=[pltpu.VMEM((BAND - 2, TILE, TILE), F32), pltpu.SemaphoreType.DMA((BAND - 2, 2))],
        input_output_aliases={3: 0},
        compiler_params=params(),
        name="band",
    )(position.reshape(1), close(v), close(rest), before)
    return pl.pallas_call(
        moved_kernel,
        out_shape=slots,
        in_specs=[SMEM, VMEM, HBM] + [VMEM] * STEPS,
        out_specs=HBM,
        scratch_shapes=[pltpu.VMEM((STEPS, TILE, TILE), F32), pltpu.SemaphoreType.DMA((STEPS, 2))],
        input_output_aliases={2: 0},
        compiler_params=params(),
        name="moved",
    )(position.reshape(1), close(v), before, *[close(x) for x in moved])


def solution(mesh):
    placed = (P(AXES, None), P(AXES), P(AXES), P())
    return jax.shard_map(
        body,
        mesh=mesh,
        in_specs=placed,
        out_specs=P(AXES, None, None, None),
        check_vma=False,
    )
```
